512 devices in a mesh: energy: 32 (over y, z_lo), atom: 16 (over x, z_hi, core).
Axes of the slice: x: 4, y: 8, z: 8 (z_hi: 2, z_lo: 4; z = z_hi * 4 + z_lo), core: 2. Of those that a mesh axis runs over, the one named last changes fastest.
Arguments:
- green_blocks: bfloat16 [256, 32, 2, 128, 128], P('atom', 'energy'), may hold values from -3 to 3
- coupling: bfloat16 [256, 3, 2, 128, 128], P('atom'), may hold values from -0.375 to 0.375
- phonon_weight: float32 [2, 256, 4], P(None, 'atom'), may hold values from 0.1 to 1
- offsets: int32 [256, 4], P('atom'), may hold values from 1 to 4, as said below
- bond_atom: int32 [256], P('atom'), may hold values from 0 to 127, as said below
Outputs:
- sigma: bfloat16 [128, 32, 2, 128, 128], P('atom', 'energy')
The draws below stay inside these ranges and needn't reach their ends.
Inputs may be any that keep to these rules, and one draw needn't show every extreme that they name: For every bond, its 4 modes' offsets are 1, 2, 3 and 4 in some order. `bond_atom`: atoms k * 8 to (k + 1) * 8 - 1 lie on index k of atom. Among the 16 bonds of one index of atom, every index of atom that is named is named by exactly 2 bonds, and one index of atom is named by 2 bonds of every index of atom.
All inputs are finite; a program needn't handle non-finite values.
Results may differ from the reference program's by a relative error of at most 0.0064.
Values may be sent and summed in bfloat16 or wider, within the bound.
A program may use at most 64 MiB of HBM per device.

```python
import math
import jax
import jax.numpy as jnp
from jax import lax

N = 128
E_DEV = 1
B_DEV = 16
A_DEV = 8
COMPONENTS = 3
MODES = 4
CAP = 2
ENERGIES = 32
BONDS = 256
ATOMS = 128
N_ATOM = 16


def draw_offsets(key, part):
    first_key, second_key = jax.random.split(jax.random.fold_in(key, 3))
    turn = jax.random.randint(first_key, (BONDS, 1), 0, MODES)
    extra = jax.random.randint(second_key, (BONDS, MODES), 0, E_DEV)
    row_index = jnp.arange(BONDS, dtype=jnp.int32)[:, None]
    extra = jnp.where(row_index == 0, E_DEV - 1, jnp.where(row_index == 1, 0, extra))
    block_index = (jnp.arange(MODES, dtype=jnp.int32)[None, :] + turn) % MODES
    return (E_DEV * block_index + 1 + extra).astype(jnp.int32)


def draw_bond_atom(key, part):
    hot_owner = jax.random.randint(jax.random.fold_in(key, 7), (), 0, N_ATOM)
    source_keys = jax.random.split(jax.random.fold_in(key, 11), N_ATOM)
    named_count = B_DEV // CAP

    def one_source(source_key):
        perm_key, order_key, atom_key = jax.random.split(source_key, 3)
        others = jax.random.permutation(perm_key, N_ATOM - 1)
        others = others + (others >= hot_owner).astype(jnp.int32)
        chosen = jnp.concatenate([hot_owner[None].astype(jnp.int32), others[:named_count - 1].astype(jnp.int32)])
        owners = jnp.repeat(chosen, CAP)
        owners = owners[jax.random.permutation(order_key, B_DEV)]
        within = jax.random.randint(atom_key, (B_DEV,), 0, A_DEV)
        return owners * A_DEV + within
    return jax.vmap(one_source)(source_keys).reshape(-1).astype(jnp.int32)


def block_levels(rng, extent, pieces, least, high):
    level, own = 1.0, jax.random.fold_in(rng, 6)
    for position, shards_of in pieces:
        draws = jnp.exp(jax.random.uniform(jax.random.fold_in(own, position), (shards_of,), jnp.float32, least / len(pieces), high / len(pieces)))
        level = level * jnp.repeat(draws, extent[position] // shards_of).reshape([-1 if axis == position else 1 for axis in range(len(extent))])
    return level


def bell_draw(key, shape, scale, most, pieces=(), held_as=jnp.bfloat16):
    loudness = block_levels(key, shape, pieces, -0.22, 0.18) if pieces else 1.0
    values = jax.random.normal(key, shape, jnp.float32) * scale * loudness
    return jnp.minimum(jnp.maximum(values, -most), most).astype(held_as)


def setup_inputs(seed: int = 0) -> dict:
    arg_keys = jax.random.split(jax.random.key(seed), 6)
    green_blocks = bell_draw(arg_keys[0], (BONDS, ENERGIES, 2, N, N), 0.5, 3.0, ((0, 16), (1, 32)))
    coupling = bell_draw(arg_keys[1], (BONDS, COMPONENTS, 2, N, N), (2 * N) ** -0.5, 0.375, ((0, 16),))
    phonon_weight = jnp.clip(jnp.exp(math.log(1.0) - 2.3025851 * jax.random.uniform(arg_keys[2], (2, BONDS, MODES), jnp.float32) ** block_levels(arg_keys[2], (2, BONDS, MODES), ((1, 16),), -0.2, 0.2)), 0.1, 1.0)
    offsets = draw_offsets(jax.random.fold_in(arg_keys[5], 71), 0)
    bond_atom = draw_bond_atom(jax.random.fold_in(arg_keys[5], 71), 0)
    return dict(green_blocks=green_blocks, coupling=coupling, phonon_weight=phonon_weight, offsets=offsets, bond_atom=bond_atom)


def mix_bond(green_bond, absorb, emit, bond_offsets):
    energy = jnp.arange(ENERGIES, dtype=jnp.int32)
    lower_index = (energy[:, None] - bond_offsets[None, :]) % ENERGIES
    upper_index = (energy[:, None] + bond_offsets[None, :]) % ENERGIES
    lower_hit = (lower_index[:, :, None] == energy[None, None, :]).astype(jnp.float32)
    upper_hit = (upper_index[:, :, None] == energy[None, None, :]).astype(jnp.float32)
    weights = jnp.sum(absorb[None, :, None] * lower_hit + emit[None, :, None] * upper_hit, axis=1)
    flat = green_bond.astype(jnp.float32).reshape(ENERGIES, -1)
    mixed = jnp.dot(weights, flat, precision=lax.Precision.HIGHEST)
    return mixed.reshape(green_bond.shape).astype(jnp.bfloat16)


def product_bond(mixed, coupling_bond):
    real_coupling = coupling_bond[:, 0].astype(jnp.float32)
    imag_coupling = coupling_bond[:, 1].astype(jnp.float32)
    real_mixed = mixed[:, 0].astype(jnp.float32)
    imag_mixed = mixed[:, 1].astype(jnp.float32)
    highest = lax.Precision.HIGHEST

    def left_mul(first, second):
        return jnp.einsum("cij,ejk->ecik", first, second, precision=highest)

    def right_mul(first, second):
        return jnp.einsum("ecij,ckj->eik", first, second, precision=highest)

    left_real = (left_mul(real_coupling, real_mixed) - left_mul(imag_coupling, imag_mixed)).astype(jnp.bfloat16)
    left_imag = (left_mul(real_coupling, imag_mixed) + left_mul(imag_coupling, real_mixed)).astype(jnp.bfloat16)
    left_real = left_real.astype(jnp.float32)
    left_imag = left_imag.astype(jnp.float32)
    out_real = right_mul(left_real, real_coupling) - right_mul(left_imag, imag_coupling)
    out_imag = right_mul(left_real, imag_coupling) + right_mul(left_imag, real_coupling)
    return jnp.stack([out_real, out_imag], axis=1).astype(jnp.bfloat16)


def reference(green_blocks, coupling, phonon_weight, offsets, bond_atom):
    def one_bond(packed):
        green_bond, coupling_bond, absorb, emit, bond_offsets = packed
        return product_bond(mix_bond(green_bond, absorb, emit, bond_offsets), coupling_bond)

    bond_self = lax.map(one_bond, (green_blocks, coupling, phonon_weight[0], phonon_weight[1], offsets))
    sigma = jax.ops.segment_sum(bond_self.astype(jnp.float32), bond_atom, num_segments=ATOMS)
    return sigma.astype(jnp.bfloat16)
```

```python
import functools

import jax
import jax.numpy as jnp
from jax import lax
from jax.experimental import pallas as pl
from jax.experimental.pallas import tpu as pltpu
from jax.sharding import PartitionSpec as P

MESH = pl.DeviceIdType.MESH
N = 128
BONDS = 16
OWNERS = 16
ATOMS = 8
MODES = 4
PARTS = 4
ROWS = N // PARTS
CHUNKS = 8
NB = BONDS // CHUNKS
STEPS = 4
STRIP = N // STEPS
BF = jnp.bfloat16
F32 = jnp.float32


def kernel(
    green, coupling, weight, offset, bond_atom, out,
    part, low, high, mixed_part, mixed, coup, bond_self,
    pack, arrived, meta, meta_in, own_sum, core_out, core_in, kept, far_out, far_in,
    slot_bond, table,
    in_send, in_recv, row_send, row_recv, back_send, back_recv, own_sem, mix_sem, coup_sem,
    meta_send, meta_recv, x_send, x_recv, core_send, core_recv, far_send, far_recv,
):
    e = lax.axis_index("energy")
    a = lax.axis_index("atom")
    y, zl = lax.div(e, PARTS), lax.rem(e, PARTS)
    x, zh, co = lax.div(a, 4), lax.rem(lax.div(a, 2), 2), lax.rem(a, 2)
    in_row = [(y * PARTS + lax.rem(zl + s, PARTS), a) for s in range(PARTS)]
    up = (lax.rem(y + 1, 8) * PARTS + zl, a)
    down = (lax.rem(y + 7, 8) * PARTS + zl, a)
    in_x = [(e, lax.rem(x + s, 4) * 4 + zh * 2 + co) for s in range(4)]
    other_core = (e, x * 4 + zh * 2 + 1 - co)
    far = (e, x * 4 + (1 - zh) * 2 + co)

    barrier = pltpu.get_barrier_semaphore()
    peers = in_row[1:] + [up, down] + in_x[1:] + [other_core, far]
    for peer in peers:
        pl.semaphore_signal(barrier, inc=1, device_id=peer, device_id_type=MESH)
    load_coup = pltpu.make_async_copy(coupling, coup, coup_sem)
    load_coup.start()
    own_load = pltpu.make_async_copy(
        green.at[:, :, pl.ds(pl.multiple_of(zl * ROWS, ROWS), ROWS), :], part.at[zl], own_sem
    )
    own_load.start()
    pl.semaphore_wait(barrier, len(peers))

    def remote(src, dst, send, recv, device):
        return pltpu.make_async_remote_copy(
            src_ref=src, dst_ref=dst, send_sem=send, recv_sem=recv, device_id=device, device_id_type=MESH
        )

    def bonds_of(q):
        return pl.ds(q * NB, NB)

    def in_copy(q, s):
        other = lax.rem(zl + s, PARTS)
        rows = pl.ds(pl.multiple_of(other * ROWS, ROWS), ROWS)
        return remote(
            green.at[bonds_of(q), :, rows, :], part.at[zl, bonds_of(q)],
            in_send.at[q, s], in_recv.at[q, zl], in_row[s],
        )

    def in_arrival(q, s):
        other = lax.rem(zl + s, PARTS)
        block = part.at[other, bonds_of(q)]
        return remote(block, block, in_send.at[q, s], in_recv.at[q, other], in_row[s])

    def row_copy(q, way):
        src = part.at[:, bonds_of(q)]
        dst = (low if way == 0 else high).at[:, bonds_of(q)]
        return remote(src, dst, row_send.at[q, way], row_recv.at[q, way], up if way == 0 else down)

    own_rows = pl.ds(pl.multiple_of(zl * ROWS, ROWS), ROWS)

    def back_copy(q, s):
        other = lax.rem(zl + s, PARTS)
        return remote(
            mixed_part.at[other, bonds_of(q)], mixed.at[bonds_of(q), :, own_rows, :],
            back_send.at[q, s], back_recv.at[q, zl], in_row[s],
        )

    def back_arrival(q, s):
        other = lax.rem(zl + s, PARTS)
        rows = pl.ds(pl.multiple_of(other * ROWS, ROWS), ROWS)
        block = mixed.at[bonds_of(q), :, rows, :]
        return remote(block, block, back_send.at[q, s], back_recv.at[q, other], in_row[s])

    def own_mixed(q):
        return pltpu.make_async_copy(
            mixed_part.at[zl, bonds_of(q)], mixed.at[bonds_of(q), :, own_rows, :], mix_sem.at[q]
        )

    @pl.loop(0, CHUNKS)
    def _(q):
        for s in (2, 1, 3):
            in_copy(q, s).start()

    @pl.loop(0, BONDS)
    def _(b):
        for d in range(1, MODES + 1):
            below = jnp.float32(0)
            above = jnp.float32(0)
            for mode in range(MODES):
                hit = offset[b, mode] == d
                below = below + jnp.where(hit, weight[0, b, mode], jnp.float32(0))
                above = above + jnp.where(hit, weight[1, b, mode], jnp.float32(0))
            table[b, d - 1] = below
            table[b, MODES + d - 1] = above

    @pl.loop(0, OWNERS)
    def _(owner):
        first = jnp.int32(BONDS)
        last = jnp.int32(-1)
        for b in range(BONDS):
            hit = lax.div(bond_atom[b], ATOMS) == owner
            first = jnp.minimum(first, jnp.where(hit, b, BONDS))
            last = jnp.maximum(last, jnp.where(hit, b, -1))
        named = last >= 0
        for place, bond in enumerate((first, last)):
            bond = jnp.clip(bond, 0, BONDS - 1)
            slot_bond[owner, place] = bond
            atom = jnp.where(named, lax.rem(bond_atom[bond], ATOMS), -1)
            meta[owner, place] = jnp.full((8, N), atom.astype(F32), F32)

    own_load.wait()

    def meta_copy(s):
        other = lax.rem(x + s, 4)
        return remote(meta.at[pl.ds(other * 4, 4)], meta_in.at[x], meta_send.at[s], meta_recv.at[x], in_x[s])

    def meta_arrival(s):
        other = lax.rem(x + s, 4)
        return remote(meta_in.at[other], meta_in.at[other], meta_send.at[s], meta_recv.at[other], in_x[s])

    def forward(q):
        for s in range(1, PARTS):
            in_arrival(q, s).wait_recv()
        row_copy(q, 0).start()
        row_copy(q, 1).start()

    def mix(q):
        row_copy(q, 0).wait_recv()
        row_copy(q, 1).wait_recv()

        @pl.loop(0, NB)
        def _(n):
            b = q * NB + n
            below = [table[b, d] for d in range(MODES)]
            above = [table[b, MODES + d] for d in range(MODES)]
            for half in range(2):
                total = [None] * PARTS

                def add(t, factor, block):
                    term = factor * block
                    total[t] = term if total[t] is None else total[t] + term

                for k in range(PARTS):
                    block = part[k, b, half].astype(F32)
                    for t in range(PARTS):
                        if k < t:
                            add(t, below[t - k - 1], block)
                        if k > t:
                            add(t, above[k - t - 1], block)
                    block = low[k, b, half].astype(F32)
                    for t in range(k + 1):
                        add(t, below[MODES - k + t - 1], block)
                    block = high[k, b, half].astype(F32)
                    for t in range(k, PARTS):
                        add(t, above[MODES + k - t - 1], block)
                for t in range(PARTS):
                    mixed_part[t, b, half] = total[t].astype(BF)

        for s in (2, 1, 3):
            back_copy(q, s).start()
        own_mixed(q).start()

    def multiply(q):
        for s in range(1, PARTS):
            back_arrival(q, s).wait_recv()
        own_mixed(q).wait()

        @pl.loop(0, NB)
        def _(n):
            b = q * NB + n
            f_re, f_im = mixed[b, 0], mixed[b, 1]
            f_all = jnp.concatenate(
                [jnp.concatenate([f_re, f_im], axis=1), jnp.concatenate([-f_im, f_re], axis=1)], axis=0
            )
            acc = jnp.zeros((N, 2 * N), F32)
            for c in range(3):
                h_re, h_im = coup[b, c, 0], coup[b, c, 1]
                h_row = jnp.concatenate([h_re, h_im], axis=1)
                left = jnp.dot(h_row, f_all, preferred_element_type=F32).astype(BF)
                h_all = jnp.concatenate(
                    [jnp.concatenate([h_re, -h_im], axis=1), jnp.concatenate([h_im, h_re], axis=1)], axis=0
                )
                acc = acc + lax.dot_general(
                    left, h_all, (((1,), (1,)), ((), ())), preferred_element_type=F32
                )
            bond_self[b, 0] = acc[:, :N].astype(BF)
            bond_self[b, 1] = acc[:, N:].astype(BF)

    forward(0)
    for s in range(1, 4):
        meta_copy(s).start()
    forward(1)
    mix(0)
    load_coup.wait()

    @pl.loop(2, CHUNKS)
    def _(q):
        forward(q)
        mix(q - 1)
        multiply(q - 2)

    mix(CHUNKS - 1)
    multiply(CHUNKS - 2)
    multiply(CHUNKS - 1)

    def x_copy(r, s):
        other = lax.rem(x + s, 4)
        return remote(
            pack.at[r, pl.ds(other * 4, 4)], arrived.at[r, x], x_send.at[r, s], x_recv.at[r, x], in_x[s]
        )

    def x_arrival(r, s):
        other = lax.rem(x + s, 4)
        block = arrived.at[r, other]
        return remote(block, block, x_send.at[r, s], x_recv.at[r, other], in_x[s])

    def core_copy(r):
        return remote(core_out.at[r], core_in.at[r], core_send.at[r], core_recv.at[r], other_core)

    def far_copy(r):
        return remote(far_out.at[r], far_in.at[r], far_send.at[r], far_recv.at[r], far)

    for r in range(STEPS):
        @pl.loop(0, OWNERS)
        def _(owner):
            for place in range(2):
                bond = slot_bond[owner, place]
                pack[r, owner, place] = bond_self[bond, :, r * STRIP : (r + 1) * STRIP, :]

        for s in (2, 1, 3):
            x_copy(r, s).start()

    for s in range(1, 4):
        meta_arrival(s).wait_recv()

    def gather(r):
        for s in range(1, 4):
            x_arrival(r, s).wait_recv()

        @pl.loop(0, 4)
        def _(turn):
            zd, other = lax.div(turn, 2), lax.rem(turn, 2)
            place_c = lax.rem(co + other, 2)
            at = zd * 2 + place_c
            for half in range(2):
                blocks = []
                names = []
                for s in range(4):
                    src = lax.rem(x + s, 4)
                    for place in range(2):
                        if s == 0:
                            blocks.append(pack[r, x * 4 + at, place, half].astype(F32))
                            names.append(meta[x * 4 + at, place])
                        else:
                            blocks.append(arrived[r, src, at, place, half].astype(F32))
                            names.append(meta_in[src, at, place])
                blocks = [v.reshape(STRIP // 8, 8, N) for v in blocks]
                for atom in range(ATOMS):
                    total = jnp.zeros((STRIP // 8, 8, N), F32)
                    for v, name in zip(blocks, names):
                        total = total + jnp.where((name == atom)[None], v, 0.0)
                    own_sum[other, zd, atom, half] = total.reshape(STRIP, N)

        core_out[r] = own_sum[1].astype(BF)
        kept[r] = own_sum[0]
        core_copy(r).start()

    def cross(r):
        core_copy(r).wait_recv()
        far_out[r] = (kept[r, 1 - zh] + core_in[r, 1 - zh].astype(F32)).astype(BF)
        kept[r, zh] = kept[r, zh] + core_in[r, zh].astype(F32)
        far_copy(r).start()

    def finish(r):
        far_copy(r).wait_recv()
        out[:, :, r * STRIP : (r + 1) * STRIP, :] = (kept[r, zh] + far_in[r].astype(F32)).astype(BF)

    for r in range(STEPS + 2):
        if r < STEPS:
            gather(r)
        if 1 <= r < STEPS + 1:
            cross(r - 1)
        if r >= 2:
            finish(r - 2)

    @pl.loop(0, CHUNKS)
    def _(q):
        for s in range(1, PARTS):
            in_copy(q, s).wait_send()
            back_copy(q, s).wait_send()
        row_copy(q, 0).wait_send()
        row_copy(q, 1).wait_send()

    for s in range(1, 4):
        meta_copy(s).wait_send()
    for r in range(STEPS):
        for s in range(1, 4):
            x_copy(r, s).wait_send()
        core_copy(r).wait_send()
        far_copy(r).wait_send()


def body(green_blocks, coupling, phonon_weight, offsets, bond_atom):
    green = green_blocks.reshape(BONDS, 2, N, N)
    vmem, smem, dma = pltpu.VMEM, pltpu.SMEM, pltpu.SemaphoreType.DMA
    any_space = pl.BlockSpec(memory_space=pl.ANY)
    small = pl.BlockSpec(memory_space=pltpu.SMEM)
    part = vmem((PARTS, BONDS, 2, ROWS, N), BF)
    out = pl.pallas_call(
        kernel,
        out_shape=jax.ShapeDtypeStruct((ATOMS, 2, N, N), BF),
        in_specs=[any_space, any_space, small, small, small],
        out_specs=pl.BlockSpec(memory_space=pltpu.VMEM),
        scratch_shapes=[
            part, part, part, part,
            vmem((BONDS, 2, N, N), BF),
            vmem((BONDS, 3, 2, N, N), BF),
            vmem((BONDS, 2, N, N), BF),
            vmem((STEPS, OWNERS, 2, 2, STRIP, N), BF),
            vmem((STEPS, 4, 4, 2, 2, STRIP, N), BF),
            vmem((OWNERS, 2, 8, N), F32),
            vmem((4, 4, 2, 8, N), F32),
            vmem((2, 2, ATOMS, 2, STRIP, N), F32),
            vmem((STEPS, 2, ATOMS, 2, STRIP, N), BF),
            vmem((STEPS, 2, ATOMS, 2, STRIP, N), BF),
            vmem((STEPS, 2, ATOMS, 2, STRIP, N), F32),
            vmem((STEPS, ATOMS, 2, STRIP, N), BF),
            vmem((STEPS, ATOMS, 2, STRIP, N), BF),
            smem((OWNERS, 2), jnp.int32),
            smem((BONDS, 2 * MODES), F32),
            dma((CHUNKS, PARTS)), dma((CHUNKS, PARTS)),
            dma((CHUNKS, 2)), dma((CHUNKS, 2)),
            dma((CHUNKS, PARTS)), dma((CHUNKS, PARTS)),
            dma, dma((CHUNKS,)), dma,
            dma((4,)), dma((4,)),
            dma((STEPS, 4)), dma((STEPS, 4)),
            dma((STEPS,)), dma((STEPS,)),
            dma((STEPS,)), dma((STEPS,)),
        ],
        compiler_params=pltpu.CompilerParams(
            collective_id=0, has_side_effects=True, vmem_limit_bytes=48 * 1024 * 1024
        ),
    )(green, coupling, phonon_weight, offsets, bond_atom)
    return out.reshape(ATOMS, 1, 2, N, N)


def solution(mesh):
    placed = (
        P("atom", "energy", None, None, None),
        P("atom", None, None, None, None),
        P(None, "atom", None),
        P("atom", None),
        P("atom"),
    )
    return jax.shard_map(
        body,
        mesh=mesh,
        in_specs=placed,
        out_specs=P("atom", "energy", None, None, None),
        check_vma=False,
    )
```

```python
import functools

import jax
import jax.numpy as jnp
from jax import lax
from jax.experimental import pallas as pl
from jax.experimental.pallas import tpu as pltpu
from jax.sharding import PartitionSpec as P

MESH = pl.DeviceIdType.MESH
N = 128
BONDS = 16
OWNERS = 16
ATOMS = 8
MODES = 4
PARTS = 4
ROWS = N // PARTS
CHUNKS = 8
NB = BONDS // CHUNKS
WINDOW = 3
PAIRS = BONDS // 2
BACK_WINDOW = 3
ORDER = (2, 1, 3)
KEYS = (2, 1, 3, 0)
STEPS = 4
STRIP = N // STEPS
BF = jnp.bfloat16
F32 = jnp.float32


def kernel(
    green, coupling, weight_in, offset_in, bond_atom_in, out,
    part, low, high, mixed_part, mixed, coup, bond_self,
    pack, arrived, meta, meta_in, core_out, core_in, kept, far_out, far_in, out_strip,
    weight, offset, bond_atom, first_of, last_of, named_at, pair_of, bond_at, table,
    small_sem, in_send, in_recv, row_send, row_recv, back_send, back_recv, own_sem, mix_sem, coup_sem,
    meta_send, meta_recv, x_send, x_recv, core_send, core_recv, far_send, far_recv, out_sem,
):
    e = lax.axis_index("energy")
    a = lax.axis_index("atom")
    y, zl = lax.div(e, PARTS), lax.rem(e, PARTS)
    x, zh, co = lax.div(a, 4), lax.rem(lax.div(a, 2), 2), lax.rem(a, 2)
    in_row = [(y * PARTS + lax.rem(zl + s, PARTS), a) for s in range(PARTS)]
    up = (lax.rem(y + 1, 8) * PARTS + zl, a)
    down = (lax.rem(y + 7, 8) * PARTS + zl, a)
    in_x = [(e, lax.rem(x + s, 4) * 4 + zh * 2 + co) for s in range(4)]
    other_core = (e, x * 4 + zh * 2 + 1 - co)
    far = (e, x * 4 + (1 - zh) * 2 + co)

    barrier = pltpu.get_barrier_semaphore()
    peers = in_row[1:] + [up, down] + in_x[1:] + [other_core, far]
    for peer in peers:
        pl.semaphore_signal(barrier, inc=1, device_id=peer, device_id_type=MESH)
    small = [
        pltpu.make_async_copy(src, dst, small_sem.at[i])
        for i, (src, dst) in enumerate(
            ((weight_in, weight), (offset_in, offset), (bond_atom_in, bond_atom))
        )
    ]
    for load in small:
        load.start()
    own_rows = pl.ds(pl.multiple_of(zl * ROWS, ROWS), ROWS)
    own_load = pltpu.make_async_copy(green.at[:, :, own_rows, :], part.at[zl], own_sem)
    own_load.start()
    load_coup = pltpu.make_async_copy(coupling, coup, coup_sem)
    load_coup.start()
    pl.semaphore_wait(barrier, len(peers))

    def remote(src, dst, send, recv, device):
        return pltpu.make_async_remote_copy(
            src_ref=src, dst_ref=dst, send_sem=send, recv_sem=recv, device_id=device, device_id_type=MESH
        )

    def rows_of(other):
        return pl.ds(pl.multiple_of(other * ROWS, ROWS), ROWS)

    def in_copy(q, s):
        bonds = pl.ds(q * NB, NB)
        return remote(
            green.at[bonds, :, rows_of(lax.rem(zl + s, PARTS)), :], part.at[zl, bonds],
            in_send.at[q, s], in_recv.at[q, zl], in_row[s],
        )

    def in_arrival(q, s):
        other = lax.rem(zl + s, PARTS)
        block = part.at[other, pl.ds(q * NB, NB)]
        return remote(block, block, in_send.at[q, s], in_recv.at[q, other], in_row[s])

    def row_copy(q, way):
        bonds = pl.ds(q * NB, NB)
        dst = (low if way == 0 else high).at[:, bonds]
        return remote(part.at[:, bonds], dst, row_send.at[q, way], row_recv.at[q, way], up if way == 0 else down)

    def back_copy(p, s):
        two = pl.ds(2 * p, 2)
        return remote(
            mixed_part.at[lax.rem(zl + s, PARTS), two], mixed.at[two, :, own_rows, :],
            back_send.at[p, s], back_recv.at[p, zl], in_row[s],
        )

    def back_arrival(p, s):
        other = lax.rem(zl + s, PARTS)
        block = mixed.at[pl.ds(2 * p, 2), :, rows_of(other), :]
        return remote(block, block, back_send.at[p, s], back_recv.at[p, other], in_row[s])

    def own_mixed(p):
        two = pl.ds(2 * p, 2)
        return pltpu.make_async_copy(mixed_part.at[zl, two], mixed.at[two, :, own_rows, :], mix_sem.at[p])

    def meta_copy(s):
        return remote(meta.at[s], meta_in.at[x], meta_send.at[s], meta_recv.at[x], in_x[s])

    def meta_arrival(s):
        block = meta_in.at[lax.rem(x + s, 4)]
        return remote(block, block, meta_send.at[s], meta_recv.at[lax.rem(x + s, 4)], in_x[s])

    def x_copy(late, kind, s):
        return remote(
            pack.at[late, kind, s], arrived.at[late, kind, x],
            x_send.at[late, kind, s], x_recv.at[late, kind, x], in_x[s],
        )

    def x_arrival(late, kind, s):
        other = lax.rem(x + s, 4)
        block = arrived.at[late, kind, other]
        return remote(block, block, x_send.at[late, kind, s], x_recv.at[late, kind, other], in_x[s])

    def core_copy(late):
        return remote(core_out.at[late], core_in.at[late], core_send.at[late], core_recv.at[late], other_core)

    def far_copy(r):
        return remote(far_out.at[r], far_in.at[r], far_send.at[r], far_recv.at[r], far)

    for q in range(WINDOW):
        for s in ORDER:
            in_copy(q, s).start()
    for load in small:
        load.wait()

    for late in range(2):
        zd = zh if late else 1 - zh
        for kind in range(2):
            for place, s in enumerate(KEYS):
                key = late * 8 + kind * 4 + place
                owner = lax.rem(x + s, 4) * 4 + zd * 2 + (co if kind else 1 - co)
                first = jnp.int32(BONDS)
                last = jnp.int32(-1)
                for b in range(BONDS):
                    hit = lax.div(bond_atom[b], ATOMS) == owner
                    first = jnp.minimum(first, jnp.where(hit, b, BONDS))
                    last = jnp.maximum(last, jnp.where(hit, b, -1))
                named = last >= 0
                first_of[key] = jnp.minimum(first, BONDS - 1)
                last_of[key] = jnp.maximum(last, 0)
                named_at[key] = jnp.where(named, 1, 0)
                for slot, bond in enumerate((first_of[key], last_of[key])):
                    atom = jnp.where(named, lax.rem(bond_atom[bond], ATOMS), -1)
                    meta[s, late, kind, slot] = jnp.full((8, N), atom.astype(F32), F32)

    def count(key, before):
        pair_of[key] = jnp.minimum(before, PAIRS - 1)
        named_at[key] = jnp.where(named_at[key] == 1, before, -1)
        return jnp.where(named_at[key] >= 0, before + 1, before)

    lax.fori_loop(0, OWNERS, count, jnp.int32(0))

    @pl.loop(0, PAIRS)
    def _(p):
        first = jnp.int32(0)
        last = jnp.int32(0)
        for key in range(OWNERS):
            hit = named_at[key] == p
            first = first + jnp.where(hit, first_of[key], 0)
            last = last + jnp.where(hit, last_of[key], 0)
        bond_at[2 * p] = first
        bond_at[2 * p + 1] = last

    @pl.loop(0, BONDS)
    def _(at):
        b = bond_at[at]
        for d in range(1, MODES + 1):
            below = jnp.float32(0)
            above = jnp.float32(0)
            for mode in range(MODES):
                hit = offset[mode, b] == d
                below = below + jnp.where(hit, weight[0, mode, b], jnp.float32(0))
                above = above + jnp.where(hit, weight[1, mode, b], jnp.float32(0))
            table[at, d - 1] = below
            table[at, MODES + d - 1] = above

    own_load.wait()

    @pl.loop(0, CHUNKS - WINDOW)
    def _(q):
        for s in range(1, PARTS):
            in_arrival(q, s).wait_recv()
        for s in ORDER:
            in_copy(q + WINDOW, s).start()
        row_copy(q, 0).start()
        row_copy(q, 1).start()

    for s in range(1, 4):
        meta_copy(s).start()

    @pl.loop(CHUNKS - WINDOW, CHUNKS)
    def _(q):
        for s in range(1, PARTS):
            in_arrival(q, s).wait_recv()
        row_copy(q, 0).start()
        row_copy(q, 1).start()

    load_coup.wait()

    @pl.loop(0, CHUNKS)
    def _(q):
        row_copy(q, 0).wait_recv()
        row_copy(q, 1).wait_recv()

    def mix(p):
        @pl.loop(0, 2)
        def _(n):
            at = 2 * p + n
            b = bond_at[at]
            below = [table[at, d] for d in range(MODES)]
            above = [table[at, MODES + d] for d in range(MODES)]
            for half in range(2):
                total = [None] * PARTS

                def add(t, factor, block):
                    term = factor * block
                    total[t] = term if total[t] is None else total[t] + term

                for k in range(PARTS):
                    block = part[k, b, half].astype(F32)
                    for t in range(PARTS):
                        if k < t:
                            add(t, below[t - k - 1], block)
                        if k > t:
                            add(t, above[k - t - 1], block)
                    block = low[k, b, half].astype(F32)
                    for t in range(k + 1):
                        add(t, below[MODES - k + t - 1], block)
                    block = high[k, b, half].astype(F32)
                    for t in range(k, PARTS):
                        add(t, above[MODES + k - t - 1], block)
                for t in range(PARTS):
                    mixed_part[t, at, half] = total[t].astype(BF)

    def send_back(p):
        for s in ORDER:
            back_copy(p, s).start()
        own_mixed(p).start()

    def multiply(p):
        for s in range(1, PARTS):
            back_arrival(p, s).wait_recv()
        own_mixed(p).wait()
        if p + BACK_WINDOW < PAIRS:
            send_back(p + BACK_WINDOW)

        @pl.loop(0, 2)
        def _(n):
            at = 2 * p + n
            b = bond_at[at]
            f_re, f_im = mixed[at, 0], mixed[at, 1]
            f_all = jnp.concatenate(
                [jnp.concatenate([f_re, f_im], axis=1), jnp.concatenate([-f_im, f_re], axis=1)], axis=0
            )
            acc = jnp.zeros((N, 2 * N), F32)
            for c in range(3):
                h_re, h_im = coup[b, c, 0], coup[b, c, 1]
                h_row = jnp.concatenate([h_re, h_im], axis=1)
                left = jnp.dot(h_row, f_all, preferred_element_type=F32).astype(BF)
                h_all = jnp.concatenate(
                    [jnp.concatenate([h_re, -h_im], axis=1), jnp.concatenate([h_im, h_re], axis=1)], axis=0
                )
                acc = acc + lax.dot_general(
                    left, h_all, (((1,), (1,)), ((), ())), preferred_element_type=F32
                )
            bond_self[at, 0] = acc[:, :N].astype(BF)
            bond_self[at, 1] = acc[:, N:].astype(BF)

    def send_key(key):
        late, kind, s = key // 8, key % 8 // 4, KEYS[key % 4]
        if s == 0:
            return
        pair = pair_of[key]
        for slot in range(2):
            pack[late, kind, s, slot] = bond_self[2 * pair + slot]
        x_copy(late, kind, s).start()

    def gather(late, kind, r, emit):
        rows = pl.ds(pl.multiple_of(r * STRIP, STRIP), STRIP)
        own = 2 * pair_of[late * 8 + kind * 4 + 3]
        for half in range(2):
            blocks = []
            names = []
            for s in range(4):
                src = lax.rem(x + s, 4)
                for slot in range(2):
                    if s == 0:
                        block = bond_self[own + slot, half, rows]
                        names.append(meta[0, late, kind, slot])
                    else:
                        block = arrived[late, kind, src, slot, half, rows]
                        names.append(meta_in[src, late, kind, slot])
                    blocks.append(block.astype(F32).reshape(STRIP // 8, 8, N))
            for atom in range(ATOMS):
                total = jnp.zeros((STRIP // 8, 8, N), F32)
                for block, name in zip(blocks, names):
                    total = total + jnp.where((name == atom)[None], block, 0.0)
                emit(atom, half, rows, total.reshape(STRIP, N))

    def gather_for_core(late):
        for s in range(1, 4):
            x_arrival(late, 0, s).wait_recv()

        @pl.loop(0, STEPS)
        def _(r):
            def emit(atom, half, rows, total):
                core_out[late, atom, half, rows] = total.astype(BF)

            gather(late, 0, r, emit)

        core_copy(late).start()

    for p in range(BACK_WINDOW):
        mix(p)
        send_back(p)
    for p in range(BACK_WINDOW, PAIRS):
        mix(p)
    for p in range(PAIRS):
        multiply(p)
        send_key(p)
        if p == PAIRS - 2:
            for s in range(1, 4):
                meta_arrival(s).wait_recv()
            gather_for_core(0)
    for key in range(8, 16):
        send_key(key)

    for s in range(1, 4):
        x_arrival(0, 1, s).wait_recv()
    core_copy(0).wait_recv()

    @pl.loop(0, STEPS)
    def _(r):
        def emit(atom, half, rows, total):
            far_out[r, atom, half] = (total + core_in[0, atom, half, rows].astype(F32)).astype(BF)

        gather(0, 1, r, emit)
        far_copy(r).start()

    gather_for_core(1)
    for s in range(1, 4):
        x_arrival(1, 1, s).wait_recv()
    core_copy(1).wait_recv()

    @pl.loop(0, STEPS)
    def _(r):
        def emit(atom, half, rows, total):
            kept[r, atom, half] = total + core_in[1, atom, half, rows].astype(F32)

        gather(1, 1, r, emit)

    def out_copy(r):
        rows = pl.ds(pl.multiple_of(r * STRIP, STRIP), STRIP)
        return pltpu.make_async_copy(out_strip.at[r], out.at[:, :, rows, :], out_sem.at[r])

    @pl.loop(0, STEPS)
    def _(r):
        far_copy(r).wait_recv()
        out_strip[r] = (kept[r] + far_in[r].astype(F32)).astype(BF)
        out_copy(r).start()

    @pl.loop(0, CHUNKS)
    def _(q):
        for s in range(1, PARTS):
            in_copy(q, s).wait_send()
        row_copy(q, 0).wait_send()
        row_copy(q, 1).wait_send()

    @pl.loop(0, PAIRS)
    def _(p):
        for s in range(1, PARTS):
            back_copy(p, s).wait_send()

    for s in range(1, 4):
        meta_copy(s).wait_send()
        for late in range(2):
            for kind in range(2):
                x_copy(late, kind, s).wait_send()
    for late in range(2):
        core_copy(late).wait_send()
    for r in range(STEPS):
        far_copy(r).wait_send()
        out_copy(r).wait()


def body(green_blocks, coupling, phonon_weight, offsets, bond_atom):
    green = green_blocks.reshape(BONDS, 2, N, N)
    vmem, smem, dma = pltpu.VMEM, pltpu.SMEM, pltpu.SemaphoreType.DMA
    any_space = pl.BlockSpec(memory_space=pl.ANY)
    part = vmem((PARTS, BONDS, 2, ROWS, N), BF)
    out = pl.pallas_call(
        kernel,
        out_shape=jax.ShapeDtypeStruct((ATOMS, 2, N, N), BF),
        in_specs=[any_space] * 5,
        out_specs=any_space,
        scratch_shapes=[
            part, part, part, part,
            vmem((BONDS, 2, N, N), BF),
            vmem((BONDS, 3, 2, N, N), BF),
            vmem((BONDS, 2, N, N), BF),
            vmem((2, 2, 4, 2, 2, N, N), BF),
            vmem((2, 2, 4, 2, 2, N, N), BF),
            vmem((4, 2, 2, 2, 8, N), F32),
            vmem((4, 2, 2, 2, 8, N), F32),
            vmem((2, ATOMS, 2, N, N), BF),
            vmem((2, ATOMS, 2, N, N), BF),
            vmem((STEPS, ATOMS, 2, STRIP, N), F32),
            vmem((STEPS, ATOMS, 2, STRIP, N), BF),
            vmem((STEPS, ATOMS, 2, STRIP, N), BF),
            vmem((STEPS, ATOMS, 2, STRIP, N), BF),
            smem((2, MODES, BONDS), F32), smem((MODES, BONDS), jnp.int32), smem((BONDS,), jnp.int32),
            smem((OWNERS,), jnp.int32), smem((OWNERS,), jnp.int32), smem((OWNERS,), jnp.int32),
            smem((OWNERS,), jnp.int32), smem((BONDS,), jnp.int32), smem((BONDS, 2 * MODES), F32),
            dma((3,)), dma((CHUNKS, PARTS)), dma((CHUNKS, PARTS)),
            dma((CHUNKS, 2)), dma((CHUNKS, 2)),
            dma((PAIRS, PARTS)), dma((PAIRS, PARTS)),
            dma, dma((PAIRS,)), dma,
            dma((4,)), dma((4,)),
            dma((2, 2, 4)), dma((2, 2, 4)),
            dma((2,)), dma((2,)),
            dma((STEPS,)), dma((STEPS,)), dma((STEPS,)),
        ],
        compiler_params=pltpu.CompilerParams(
            collective_id=0, has_side_effects=True, vmem_limit_bytes=63 * 1024 * 1024
        ),
    )(green, coupling, phonon_weight.transpose(0, 2, 1), offsets.T, bond_atom)
    return out.reshape(ATOMS, 1, 2, N, N)


def solution(mesh):
    placed = (
        P("atom", "energy", None, None, None),
        P("atom", None, None, None, None),
        P(None, "atom", None),
        P("atom", None),
        P("atom"),
    )
    return jax.shard_map(
        body,
        mesh=mesh,
        in_specs=placed,
        out_specs=P("atom", "energy", None, None, None),
        check_vma=False,
    )
```

```python
import functools

import jax
import jax.numpy as jnp
from jax import lax
from jax.experimental import pallas as pl
from jax.experimental.pallas import tpu as pltpu
from jax.sharding import PartitionSpec as P

MESH = pl.DeviceIdType.MESH
N = 128
BONDS = 16
OWNERS = 16
ATOMS = 8
MODES = 4
PARTS = 4
ROWS = N // PARTS
CHUNKS = 8
NB = BONDS // CHUNKS
WINDOW = 2
PAIRS = BONDS // 2
BACK_WINDOW = 3
EARLY = 2
ORDER = (2, 1, 3)
KEYS = (2, 1, 3)
STEPS = 4
STRIP = N // STEPS
BF = jnp.bfloat16
F32 = jnp.float32


def key_index(late, kind, s):
    return late * 8 + (kind * 3 + KEYS.index(s) if s else 6 + kind)


def kernel(
    green, coupling, weight_in, offset_in, bond_atom_in, out,
    part, low, high, mixed_part, mixed, coup, bond_self,
    pack, arrived, meta, meta_in, core_out, core_in, kept, far_out, far_in, out_strip,
    weight, offset, bond_atom, key_of, place_of, bond_at, slot_at, table,
    small_sem, in_send, in_recv, row_send, row_recv, back_send, back_recv, own_sem, mix_sem, coup_sem,
    meta_send, meta_recv, x_send, x_recv, core_send, core_recv, far_send, far_recv, out_sem,
):
    e = lax.axis_index("energy")
    a = lax.axis_index("atom")
    y, zl = lax.div(e, PARTS), lax.rem(e, PARTS)
    x, zh, co = lax.div(a, 4), lax.rem(lax.div(a, 2), 2), lax.rem(a, 2)
    in_row = [(y * PARTS + lax.rem(zl + s, PARTS), a) for s in range(PARTS)]
    up = (lax.rem(y + 1, 8) * PARTS + zl, a)
    down = (lax.rem(y + 7, 8) * PARTS + zl, a)
    in_x = [(e, lax.rem(x + s, 4) * 4 + zh * 2 + co) for s in range(4)]
    other_core = (e, x * 4 + zh * 2 + 1 - co)
    far = (e, x * 4 + (1 - zh) * 2 + co)

    barrier = pltpu.get_barrier_semaphore()
    peers = in_row[1:] + [up, down] + in_x[1:] + [other_core, far]
    for peer in peers:
        pl.semaphore_signal(barrier, inc=1, device_id=peer, device_id_type=MESH)
    small = [
        pltpu.make_async_copy(src, dst, small_sem.at[i])
        for i, (src, dst) in enumerate(
            ((weight_in, weight), (offset_in, offset), (bond_atom_in, bond_atom))
        )
    ]
    for load in small:
        load.start()
    own_rows = pl.ds(pl.multiple_of(zl * ROWS, ROWS), ROWS)
    own_load = pltpu.make_async_copy(green.at[:, :, own_rows, :], part.at[zl], own_sem)
    own_load.start()
    load_coup = pltpu.make_async_copy(coupling, coup, coup_sem)
    load_coup.start()
    pl.semaphore_wait(barrier, len(peers))

    def remote(src, dst, send, recv, device):
        return pltpu.make_async_remote_copy(
            src_ref=src, dst_ref=dst, send_sem=send, recv_sem=recv, device_id=device, device_id_type=MESH
        )

    def rows_of(other):
        return pl.ds(pl.multiple_of(other * ROWS, ROWS), ROWS)

    def in_copy(q, s):
        bonds = pl.ds(q * NB, NB)
        return remote(
            green.at[bonds, :, rows_of(lax.rem(zl + s, PARTS)), :], part.at[zl, bonds],
            in_send.at[q, s], in_recv.at[q, zl], in_row[s],
        )

    def in_arrival(q, s):
        other = lax.rem(zl + s, PARTS)
        block = part.at[other, pl.ds(q * NB, NB)]
        return remote(block, block, in_send.at[q, s], in_recv.at[q, other], in_row[s])

    def row_copy(q, way):
        bonds = pl.ds(q * NB, NB)
        dst = (low if way == 0 else high).at[:, bonds]
        return remote(part.at[:, bonds], dst, row_send.at[q, way], row_recv.at[q, way], up if way == 0 else down)

    def back_copy(p, s):
        two = pl.ds(2 * p, 2)
        return remote(
            mixed_part.at[lax.rem(zl + s, PARTS), two], mixed.at[two, :, own_rows, :],
            back_send.at[p, s], back_recv.at[p, zl], in_row[s],
        )

    def back_arrival(p, s):
        other = lax.rem(zl + s, PARTS)
        block = mixed.at[pl.ds(2 * p, 2), :, rows_of(other), :]
        return remote(block, block, back_send.at[p, s], back_recv.at[p, other], in_row[s])

    def own_mixed(p):
        two = pl.ds(2 * p, 2)
        return pltpu.make_async_copy(mixed_part.at[zl, two], mixed.at[two, :, own_rows, :], mix_sem.at[p])

    def meta_copy(s):
        return remote(meta.at[s], meta_in.at[x], meta_send.at[s], meta_recv.at[x], in_x[s])

    def meta_arrival(s):
        block = meta_in.at[lax.rem(x + s, 4)]
        return remote(block, block, meta_send.at[s], meta_recv.at[lax.rem(x + s, 4)], in_x[s])

    def x_copy(late, kind, s):
        return remote(
            pack.at[late, kind, s], arrived.at[late, kind, x],
            x_send.at[late, kind, s], x_recv.at[late, kind, x], in_x[s],
        )

    def x_arrival(late, kind, s):
        other = lax.rem(x + s, 4)
        block = arrived.at[late, kind, other]
        return remote(block, block, x_send.at[late, kind, s], x_recv.at[late, kind, other], in_x[s])

    def core_copy(late, r):
        return remote(
            core_out.at[late, r], core_in.at[late, r], core_send.at[late, r], core_recv.at[late, r], other_core
        )

    def far_copy(r):
        return remote(far_out.at[r], far_in.at[r], far_send.at[r], far_recv.at[r], far)

    for q in range(WINDOW):
        for s in ORDER:
            in_copy(q, s).start()
    for load in small:
        load.wait()

    @pl.loop(0, BONDS)
    def _(b):
        owner = lax.div(bond_atom[b], ATOMS)
        turn = lax.rem(lax.div(owner, 4) + 4 - x, 4)
        place = jnp.where(turn == 2, 0, jnp.where(turn == 1, 1, 2))
        late = jnp.where(lax.rem(lax.div(owner, 2), 2) == zh, 8, 0)
        kind = jnp.where(lax.rem(owner, 2) == co, 1, 0)
        key_of[b] = late + jnp.where(turn == 0, 6 + kind, 3 * kind + place)
        place_of[b] = b

    @pl.loop(EARLY, BONDS)
    def _(b):
        mine = key_of[b] * BONDS + b
        rank = jnp.int32(EARLY)
        for other in range(EARLY, BONDS):
            rank = rank + jnp.where(key_of[other] * BONDS + other < mine, 1, 0)
        place_of[b] = rank

    @pl.loop(0, BONDS)
    def _(at):
        found = jnp.int32(0)
        for b in range(BONDS):
            found = found + jnp.where(place_of[b] == at, b, 0)
        bond_at[at] = found

    for late in range(2):
        for kind in range(2):
            for s in range(4):
                key = key_index(late, kind, s)
                first = jnp.int32(BONDS)
                last = jnp.int32(-1)
                for b in range(BONDS):
                    hit = key_of[b] == key
                    first = jnp.minimum(first, jnp.where(hit, b, BONDS))
                    last = jnp.maximum(last, jnp.where(hit, b, -1))
                named = last >= 0
                for slot, bond in enumerate((first, last)):
                    bond = jnp.minimum(jnp.maximum(bond, 0), BONDS - 1)
                    slot_at[key, slot] = jnp.where(named, place_of[bond], 0)
                    atom = jnp.where(named, lax.rem(bond_atom[bond], ATOMS), -1)
                    meta[s, late, kind, slot] = jnp.full((8, N), atom.astype(F32), F32)

    @pl.loop(0, BONDS)
    def _(at):
        b = bond_at[at]
        for d in range(1, MODES + 1):
            below = jnp.float32(0)
            above = jnp.float32(0)
            for mode in range(MODES):
                hit = offset[mode, b] == d
                below = below + jnp.where(hit, weight[0, mode, b], jnp.float32(0))
                above = above + jnp.where(hit, weight[1, mode, b], jnp.float32(0))
            table[at, d - 1] = below
            table[at, MODES + d - 1] = above

    own_load.wait()

    @pl.loop(0, CHUNKS - WINDOW)
    def _(q):
        for s in range(1, PARTS):
            in_arrival(q, s).wait_recv()
        for s in ORDER:
            in_copy(q + WINDOW, s).start()
        row_copy(q, 0).start()
        row_copy(q, 1).start()

    for s in range(1, 4):
        meta_copy(s).start()

    @pl.loop(CHUNKS - WINDOW, CHUNKS)
    def _(q):
        for s in range(1, PARTS):
            in_arrival(q, s).wait_recv()
        row_copy(q, 0).start()
        row_copy(q, 1).start()

    def mix(p):
        @pl.loop(0, 2)
        def _(n):
            at = 2 * p + n
            b = at if p < EARLY // 2 else bond_at[at]
            below = [table[at, d] for d in range(MODES)]
            above = [table[at, MODES + d] for d in range(MODES)]
            for half in range(2):
                total = [None] * PARTS

                def add(t, factor, block):
                    term = factor * block
                    total[t] = term if total[t] is None else total[t] + term

                for k in range(PARTS):
                    block = part[k, b, half].astype(F32)
                    for t in range(PARTS):
                        if k < t:
                            add(t, below[t - k - 1], block)
                        if k > t:
                            add(t, above[k - t - 1], block)
                    block = low[k, b, half].astype(F32)
                    for t in range(k + 1):
                        add(t, below[MODES - k + t - 1], block)
                    block = high[k, b, half].astype(F32)
                    for t in range(k, PARTS):
                        add(t, above[MODES + k - t - 1], block)
                for t in range(PARTS):
                    mixed_part[t, at, half] = total[t].astype(BF)

    def send_back(p):
        for s in ORDER:
            back_copy(p, s).start()
        own_mixed(p).start()

    def multiply(p):
        for s in range(1, PARTS):
            back_arrival(p, s).wait_recv()
        own_mixed(p).wait()
        if p + BACK_WINDOW < PAIRS:
            send_back(p + BACK_WINDOW)

        @pl.loop(0, 2)
        def _(n):
            at = 2 * p + n
            b = bond_at[at]
            f_re, f_im = mixed[at, 0], mixed[at, 1]
            f_all = jnp.concatenate(
                [jnp.concatenate([f_re, f_im], axis=1), jnp.concatenate([-f_im, f_re], axis=1)], axis=0
            )
            acc = jnp.zeros((N, 2 * N), F32)
            for c in range(3):
                h_re, h_im = coup[b, c, 0], coup[b, c, 1]
                h_row = jnp.concatenate([h_re, h_im], axis=1)
                left = jnp.dot(h_row, f_all, preferred_element_type=F32).astype(BF)
                h_all = jnp.concatenate(
                    [jnp.concatenate([h_re, -h_im], axis=1), jnp.concatenate([h_im, h_re], axis=1)], axis=0
                )
                acc = acc + lax.dot_general(
                    left, h_all, (((1,), (1,)), ((), ())), preferred_element_type=F32
                )
            bond_self[at, 0] = acc[:, :N].astype(BF)
            bond_self[at, 1] = acc[:, N:].astype(BF)

    def send_key(late, kind, s):
        key = key_index(late, kind, s)
        for slot in range(2):
            pack[late, kind, s, slot] = bond_self[slot_at[key, slot]]
        x_copy(late, kind, s).start()

    def gather(late, kind, r, emit):
        rows = pl.ds(pl.multiple_of(r * STRIP, STRIP), STRIP)
        own = key_index(late, kind, 0)
        for half in range(2):
            blocks = []
            names = []
            for s in range(4):
                src = lax.rem(x + s, 4)
                for slot in range(2):
                    if s == 0:
                        block = bond_self[slot_at[own, slot], half, rows]
                        names.append(meta[0, late, kind, slot])
                    else:
                        block = arrived[late, kind, src, slot, half, rows]
                        names.append(meta_in[src, late, kind, slot])
                    blocks.append(block.astype(F32).reshape(STRIP // 8, 8, N))
            for atom in range(ATOMS):
                total = jnp.zeros((STRIP // 8, 8, N), F32)
                for block, name in zip(blocks, names):
                    total = total + jnp.where((name == atom)[None], block, 0.0)
                emit(atom, half, rows, total.reshape(STRIP, N))

    def gather_for_core(late):
        for s in range(1, 4):
            x_arrival(late, 0, s).wait_recv()

        @pl.loop(0, STEPS)
        def _(r):
            def emit(atom, half, rows, total):
                core_out[late, r, atom, half] = total.astype(BF)

            gather(late, 0, r, emit)
            core_copy(late, r).start()

    def rows_arrived(q):
        row_copy(q, 0).wait_recv()
        row_copy(q, 1).wait_recv()

    for q in range(EARLY // NB):
        rows_arrived(q)
    for p in range(EARLY // 2):
        mix(p)
        send_back(p)
    load_coup.wait()

    @pl.loop(EARLY // NB, CHUNKS)
    def _(q):
        rows_arrived(q)

    for p in range(EARLY // 2, BACK_WINDOW):
        mix(p)
        send_back(p)
    for p in range(BACK_WINDOW, PAIRS):
        mix(p)
    for p in range(PAIRS):
        multiply(p)
        for kind in range(2):
            for s in KEYS:
                if p == min(key_index(0, kind, s) + EARLY // 2, PAIRS - 1):
                    send_key(0, kind, s)
    for s in range(1, 4):
        meta_arrival(s).wait_recv()
    gather_for_core(0)
    for s in range(1, 4):
        x_arrival(0, 1, s).wait_recv()

    @pl.loop(0, STEPS)
    def _(r):
        def emit(atom, half, rows, total):
            far_out[r, atom, half] = (total + core_in[0, r, atom, half].astype(F32)).astype(BF)

        core_copy(0, r).wait_recv()
        gather(0, 1, r, emit)
        far_copy(r).start()

    for kind in range(2):
        for s in KEYS:
            send_key(1, kind, s)
    gather_for_core(1)
    for s in range(1, 4):
        x_arrival(1, 1, s).wait_recv()

    @pl.loop(0, STEPS)
    def _(r):
        def emit(atom, half, rows, total):
            kept[r, atom, half] = total + core_in[1, r, atom, half].astype(F32)

        core_copy(1, r).wait_recv()
        gather(1, 1, r, emit)

    def out_copy(r):
        rows = pl.ds(pl.multiple_of(r * STRIP, STRIP), STRIP)
        return pltpu.make_async_copy(out_strip.at[r], out.at[:, :, rows, :], out_sem.at[r])

    @pl.loop(0, STEPS)
    def _(r):
        far_copy(r).wait_recv()
        out_strip[r] = (kept[r] + far_in[r].astype(F32)).astype(BF)
        out_copy(r).start()

    @pl.loop(0, CHUNKS)
    def _(q):
        for s in range(1, PARTS):
            in_copy(q, s).wait_send()
        row_copy(q, 0).wait_send()
        row_copy(q, 1).wait_send()

    @pl.loop(0, PAIRS)
    def _(p):
        for s in range(1, PARTS):
            back_copy(p, s).wait_send()

    for s in range(1, 4):
        meta_copy(s).wait_send()
        for late in range(2):
            for kind in range(2):
                x_copy(late, kind, s).wait_send()
    for r in range(STEPS):
        for late in range(2):
            core_copy(late, r).wait_send()
        far_copy(r).wait_send()
        out_copy(r).wait()


def body(green_blocks, coupling, phonon_weight, offsets, bond_atom):
    green = green_blocks.reshape(BONDS, 2, N, N)
    vmem, smem, dma = pltpu.VMEM, pltpu.SMEM, pltpu.SemaphoreType.DMA
    any_space = pl.BlockSpec(memory_space=pl.ANY)
    part = vmem((PARTS, BONDS, 2, ROWS, N), BF)
    out = pl.pallas_call(
        kernel,
        out_shape=jax.ShapeDtypeStruct((ATOMS, 2, N, N), BF),
        in_specs=[any_space] * 5,
        out_specs=any_space,
        scratch_shapes=[
            part, part, part, part,
            vmem((BONDS, 2, N, N), BF),
            vmem((BONDS, 3, 2, N, N), BF),
            vmem((BONDS, 2, N, N), BF),
            vmem((2, 2, 4, 2, 2, N, N), BF),
            vmem((2, 2, 4, 2, 2, N, N), BF),
            vmem((4, 2, 2, 2, 8, N), F32),
            vmem((4, 2, 2, 2, 8, N), F32),
            vmem((2, STEPS, ATOMS, 2, STRIP, N), BF),
            vmem((2, STEPS, ATOMS, 2, STRIP, N), BF),
            vmem((STEPS, ATOMS, 2, STRIP, N), F32),
            vmem((STEPS, ATOMS, 2, STRIP, N), BF),
            vmem((STEPS, ATOMS, 2, STRIP, N), BF),
            vmem((STEPS, ATOMS, 2, STRIP, N), BF),
            smem((2, MODES, BONDS), F32), smem((MODES, BONDS), jnp.int32), smem((BONDS,), jnp.int32),
            smem((BONDS,), jnp.int32), smem((BONDS,), jnp.int32), smem((BONDS,), jnp.int32),
            smem((OWNERS, 2), jnp.int32), smem((BONDS, 2 * MODES), F32),
            dma((3,)), dma((CHUNKS, PARTS)), dma((CHUNKS, PARTS)),
            dma((CHUNKS, 2)), dma((CHUNKS, 2)),
            dma((PAIRS, PARTS)), dma((PAIRS, PARTS)),
            dma, dma((PAIRS,)), dma,
            dma((4,)), dma((4,)),
            dma((2, 2, 4)), dma((2, 2, 4)),
            dma((2, STEPS)), dma((2, STEPS)),
            dma((STEPS,)), dma((STEPS,)), dma((STEPS,)),
        ],
        compiler_params=pltpu.CompilerParams(
            collective_id=0, has_side_effects=True, vmem_limit_bytes=63 * 1024 * 1024
        ),
    )(green, coupling, phonon_weight.transpose(0, 2, 1), offsets.T, bond_atom)
    return out.reshape(ATOMS, 1, 2, N, N)


def solution(mesh):
    placed = (
        P("atom", "energy", None, None, None),
        P("atom", None, None, None, None),
        P(None, "atom", None),
        P("atom", None),
        P("atom"),
    )
    return jax.shard_map(
        body,
        mesh=mesh,
        in_specs=placed,
        out_specs=P("atom", "energy", None, None, None),
        check_vma=False,
    )
```

```python
import functools

import jax
import jax.numpy as jnp
from jax import lax
from jax.experimental import pallas as pl
from jax.experimental.pallas import tpu as pltpu
from jax.sharding import PartitionSpec as P

MESH = pl.DeviceIdType.MESH
N = 128
BONDS = 16
OWNERS = 16
ATOMS = 8
MODES = 4
PARTS = 4
ROWS = N // PARTS
CHUNKS = 8
NB = BONDS // CHUNKS
WINDOW = 2
PAIRS = BONDS // 2
BACK_WINDOW = 3
EARLY = 2
ORDER = (2, 1, 3)
KEYS = (2, 1, 3)
STEPS = 4
STRIP = N // STEPS
BF = jnp.bfloat16
F32 = jnp.float32


def key_index(late, kind, s):
    return late * 8 + (kind * 3 + KEYS.index(s) if s else 6 + kind)


def kernel(
    green, coupling, weight_in, offset_in, bond_atom_in, out,
    part, low, high, mixed_part, mixed, coup, bond_self,
    pack, arrived, meta, meta_in, core_out, core_in, kept, far_out, far_in, out_strip,
    weight, offset, bond_atom, key_of, place_of, bond_at, slot_at, table,
    small_sem, in_send, in_recv, row_send, row_recv, back_send, back_recv, own_sem, mix_sem, coup_sem,
    meta_send, meta_recv, x_send, x_recv, core_send, core_recv, far_send, far_recv, out_sem,
):
    e = lax.axis_index("energy")
    a = lax.axis_index("atom")
    y, zl = lax.div(e, PARTS), lax.rem(e, PARTS)
    x, zh, co = lax.div(a, 4), lax.rem(lax.div(a, 2), 2), lax.rem(a, 2)
    in_row = [(y * PARTS + lax.rem(zl + s, PARTS), a) for s in range(PARTS)]
    up = (lax.rem(y + 1, 8) * PARTS + zl, a)
    down = (lax.rem(y + 7, 8) * PARTS + zl, a)
    in_x = [(e, lax.rem(x + s, 4) * 4 + zh * 2 + co) for s in range(4)]
    other_core = (e, x * 4 + zh * 2 + 1 - co)
    far = (e, x * 4 + (1 - zh) * 2 + co)

    barrier = pltpu.get_barrier_semaphore()
    peers = in_row[1:] + [up, down] + in_x[1:] + [other_core, far]
    for peer in peers:
        pl.semaphore_signal(barrier, inc=1, device_id=peer, device_id_type=MESH)
    small = [
        pltpu.make_async_copy(src, dst, small_sem.at[i])
        for i, (src, dst) in enumerate(
            ((weight_in, weight), (offset_in, offset), (bond_atom_in, bond_atom))
        )
    ]
    for load in small:
        load.start()
    own_rows = pl.ds(pl.multiple_of(zl * ROWS, ROWS), ROWS)
    own_load = pltpu.make_async_copy(green.at[:, :, own_rows, :], part.at[zl], own_sem)
    own_load.start()
    load_coup = pltpu.make_async_copy(coupling, coup, coup_sem)
    load_coup.start()
    pl.semaphore_wait(barrier, len(peers))

    def remote(src, dst, send, recv, device):
        return pltpu.make_async_remote_copy(
            src_ref=src, dst_ref=dst, send_sem=send, recv_sem=recv, device_id=device, device_id_type=MESH
        )

    def rows_of(other):
        return pl.ds(pl.multiple_of(other * ROWS, ROWS), ROWS)

    def in_copy(q, s):
        bonds = pl.ds(q * NB, NB)
        return remote(
            green.at[bonds, :, rows_of(lax.rem(zl + s, PARTS)), :], part.at[zl, bonds],
            in_send.at[q, s], in_recv.at[q, zl], in_row[s],
        )

    def in_arrival(q, s):
        other = lax.rem(zl + s, PARTS)
        block = part.at[other, pl.ds(q * NB, NB)]
        return remote(block, block, in_send.at[q, s], in_recv.at[q, other], in_row[s])

    def row_copy(q, way):
        bonds = pl.ds(q * NB, NB)
        dst = (low if way == 0 else high).at[:, bonds]
        return remote(part.at[:, bonds], dst, row_send.at[q, way], row_recv.at[q, way], up if way == 0 else down)

    def back_copy(p, s):
        two = pl.ds(2 * p, 2)
        return remote(
            mixed_part.at[lax.rem(zl + s, PARTS), two], mixed.at[two, :, own_rows, :],
            back_send.at[p, s], back_recv.at[p, zl], in_row[s],
        )

    def back_arrival(p, s):
        other = lax.rem(zl + s, PARTS)
        block = mixed.at[pl.ds(2 * p, 2), :, rows_of(other), :]
        return remote(block, block, back_send.at[p, s], back_recv.at[p, other], in_row[s])

    def own_mixed(p):
        two = pl.ds(2 * p, 2)
        return pltpu.make_async_copy(mixed_part.at[zl, two], mixed.at[two, :, own_rows, :], mix_sem.at[p])

    def meta_copy(s):
        return remote(meta.at[s], meta_in.at[x], meta_send.at[s], meta_recv.at[x], in_x[s])

    def meta_arrival(s):
        block = meta_in.at[lax.rem(x + s, 4)]
        return remote(block, block, meta_send.at[s], meta_recv.at[lax.rem(x + s, 4)], in_x[s])

    def x_copy(late, kind, s):
        return remote(
            pack.at[late, kind, s], arrived.at[late, kind, x],
            x_send.at[late, kind, s], x_recv.at[late, kind, x], in_x[s],
        )

    def x_arrival(late, kind, s):
        other = lax.rem(x + s, 4)
        block = arrived.at[late, kind, other]
        return remote(block, block, x_send.at[late, kind, s], x_recv.at[late, kind, other], in_x[s])

    def core_copy(late, r):
        return remote(
            core_out.at[late, r], core_in.at[late, r], core_send.at[late, r], core_recv.at[late, r], other_core
        )

    def far_copy(r):
        return remote(far_out.at[r], far_in.at[r], far_send.at[r], far_recv.at[r], far)

    for q in range(WINDOW):
        for s in ORDER:
            in_copy(q, s).start()
    def find_keys():
        for load in small:
            load.wait()


        @pl.loop(0, BONDS)
        def _(b):
            owner = lax.div(bond_atom[b], ATOMS)
            turn = lax.rem(lax.div(owner, 4) + 4 - x, 4)
            place = jnp.where(turn == 2, 0, jnp.where(turn == 1, 1, 2))
            late = jnp.where(lax.rem(lax.div(owner, 2), 2) == zh, 8, 0)
            kind = jnp.where(lax.rem(owner, 2) == co, 1, 0)
            key_of[b] = late + jnp.where(turn == 0, 6 + kind, 3 * kind + place)
            place_of[b] = b

        @pl.loop(EARLY, BONDS)
        def _(b):
            mine = key_of[b] * BONDS + b
            rank = jnp.int32(EARLY)
            for other in range(EARLY, BONDS):
                rank = rank + jnp.where(key_of[other] * BONDS + other < mine, 1, 0)
            place_of[b] = rank

    def find_bonds():
        @pl.loop(0, BONDS)
        def _(at):
            found = jnp.int32(0)
            for b in range(BONDS):
                found = found + jnp.where(place_of[b] == at, b, 0)
            bond_at[at] = found

    def find_slots(lates):
        for late in lates:
            for kind in range(2):
                for s in range(4):
                    key = key_index(late, kind, s)
                    first = jnp.int32(BONDS)
                    last = jnp.int32(-1)
                    for b in range(BONDS):
                        hit = key_of[b] == key
                        first = jnp.minimum(first, jnp.where(hit, b, BONDS))
                        last = jnp.maximum(last, jnp.where(hit, b, -1))
                    named = last >= 0
                    for slot, bond in enumerate((first, last)):
                        bond = jnp.minimum(jnp.maximum(bond, 0), BONDS - 1)
                        slot_at[key, slot] = jnp.where(named, place_of[bond], 0)
                        atom = jnp.where(named, lax.rem(bond_atom[bond], ATOMS), -1)
                        meta[s, late, kind, slot] = jnp.full((8, N), atom.astype(F32), F32)

    def find_factors():
        @pl.loop(0, BONDS)
        def _(at):
            b = bond_at[at]
            for d in range(1, MODES + 1):
                below = jnp.float32(0)
                above = jnp.float32(0)
                for mode in range(MODES):
                    hit = offset[mode, b] == d
                    below = below + jnp.where(hit, weight[0, mode, b], jnp.float32(0))
                    above = above + jnp.where(hit, weight[1, mode, b], jnp.float32(0))
                table[at, d - 1] = below
                table[at, MODES + d - 1] = above

    own_load.wait()

    tasks = (
        find_keys, find_bonds, functools.partial(find_slots, (0,)), functools.partial(find_slots, (1,)), find_factors,
    )
    for q in range(CHUNKS - WINDOW):
        for s in range(1, PARTS):
            in_arrival(q, s).wait_recv()
        for s in ORDER:
            in_copy(q + WINDOW, s).start()
        row_copy(q, 0).start()
        row_copy(q, 1).start()
        if q < len(tasks):
            tasks[q]()

    for s in range(1, 4):
        meta_copy(s).start()

    @pl.loop(CHUNKS - WINDOW, CHUNKS)
    def _(q):
        for s in range(1, PARTS):
            in_arrival(q, s).wait_recv()
        row_copy(q, 0).start()
        row_copy(q, 1).start()

    def mix(p):
        @pl.loop(0, 2)
        def _(n):
            at = 2 * p + n
            b = at if p < EARLY // 2 else bond_at[at]
            below = [table[at, d] for d in range(MODES)]
            above = [table[at, MODES + d] for d in range(MODES)]
            for half in range(2):
                total = [None] * PARTS

                def add(t, factor, block):
                    term = factor * block
                    total[t] = term if total[t] is None else total[t] + term

                for k in range(PARTS):
                    block = part[k, b, half].astype(F32)
                    for t in range(PARTS):
                        if k < t:
                            add(t, below[t - k - 1], block)
                        if k > t:
                            add(t, above[k - t - 1], block)
                    block = low[k, b, half].astype(F32)
                    for t in range(k + 1):
                        add(t, below[MODES - k + t - 1], block)
                    block = high[k, b, half].astype(F32)
                    for t in range(k, PARTS):
                        add(t, above[MODES + k - t - 1], block)
                for t in range(PARTS):
                    mixed_part[t, at, half] = total[t].astype(BF)

    def send_back(p):
        for s in ORDER:
            back_copy(p, s).start()
        own_mixed(p).start()

    def multiply(p):
        for s in range(1, PARTS):
            back_arrival(p, s).wait_recv()
        own_mixed(p).wait()
        if p + BACK_WINDOW < PAIRS:
            send_back(p + BACK_WINDOW)

        @pl.loop(0, 2)
        def _(n):
            at = 2 * p + n
            b = bond_at[at]
            f_re, f_im = mixed[at, 0], mixed[at, 1]
            f_all = jnp.concatenate(
                [jnp.concatenate([f_re, f_im], axis=1), jnp.concatenate([-f_im, f_re], axis=1)], axis=0
            )
            acc = jnp.zeros((N, 2 * N), F32)
            for c in range(3):
                h_re, h_im = coup[b, c, 0], coup[b, c, 1]
                h_row = jnp.concatenate([h_re, h_im], axis=1)
                left = jnp.dot(h_row, f_all, preferred_element_type=F32).astype(BF)
                h_all = jnp.concatenate(
                    [jnp.concatenate([h_re, -h_im], axis=1), jnp.concatenate([h_im, h_re], axis=1)], axis=0
                )
                acc = acc + lax.dot_general(
                    left, h_all, (((1,), (1,)), ((), ())), preferred_element_type=F32
                )
            bond_self[at, 0] = acc[:, :N].astype(BF)
            bond_self[at, 1] = acc[:, N:].astype(BF)

    def send_key(late, kind, s):
        key = key_index(late, kind, s)
        for slot in range(2):
            pack[late, kind, s, slot] = bond_self[slot_at[key, slot]]
        x_copy(late, kind, s).start()

    def gather(late, kind, r, emit):
        rows = pl.ds(pl.multiple_of(r * STRIP, STRIP), STRIP)
        own = key_index(late, kind, 0)
        for half in range(2):
            blocks = []
            names = []
            for s in range(4):
                src = lax.rem(x + s, 4)
                for slot in range(2):
                    if s == 0:
                        block = bond_self[slot_at[own, slot], half, rows]
                        names.append(meta[0, late, kind, slot])
                    else:
                        block = arrived[late, kind, src, slot, half, rows]
                        names.append(meta_in[src, late, kind, slot])
                    blocks.append(block.astype(F32).reshape(STRIP // 8, 8, N))
            for atom in range(ATOMS):
                total = jnp.zeros((STRIP // 8, 8, N), F32)
                for block, name in zip(blocks, names):
                    total = total + jnp.where((name == atom)[None], block, 0.0)
                emit(atom, half, rows, total.reshape(STRIP, N))

    def gather_for_core(late):
        for s in range(1, 4):
            x_arrival(late, 0, s).wait_recv()

        @pl.loop(0, STEPS)
        def _(r):
            def emit(atom, half, rows, total):
                core_out[late, r, atom, half] = total.astype(BF)

            gather(late, 0, r, emit)
            core_copy(late, r).start()

    def rows_arrived(q):
        row_copy(q, 0).wait_recv()
        row_copy(q, 1).wait_recv()

    for q in range(EARLY // NB):
        rows_arrived(q)
    for p in range(EARLY // 2):
        mix(p)
        send_back(p)
    load_coup.wait()

    @pl.loop(EARLY // NB, CHUNKS)
    def _(q):
        rows_arrived(q)

    for p in range(EARLY // 2, BACK_WINDOW):
        mix(p)
        send_back(p)
    for p in range(BACK_WINDOW, PAIRS):
        mix(p)
    for p in range(PAIRS):
        multiply(p)
        for kind in range(2):
            for s in KEYS:
                if p == min(key_index(0, kind, s) + EARLY // 2, PAIRS - 1):
                    send_key(0, kind, s)
    for s in range(1, 4):
        meta_arrival(s).wait_recv()
    gather_for_core(0)
    for s in range(1, 4):
        x_arrival(0, 1, s).wait_recv()

    @pl.loop(0, STEPS)
    def _(r):
        def emit(atom, half, rows, total):
            far_out[r, atom, half] = (total + core_in[0, r, atom, half].astype(F32)).astype(BF)

        core_copy(0, r).wait_recv()
        gather(0, 1, r, emit)
        far_copy(r).start()

    for kind in range(2):
        for s in KEYS:
            send_key(1, kind, s)
    gather_for_core(1)
    for s in range(1, 4):
        x_arrival(1, 1, s).wait_recv()

    @pl.loop(0, STEPS)
    def _(r):
        def emit(atom, half, rows, total):
            kept[r, atom, half] = total + core_in[1, r, atom, half].astype(F32)

        core_copy(1, r).wait_recv()
        gather(1, 1, r, emit)

    def out_copy(r):
        rows = pl.ds(pl.multiple_of(r * STRIP, STRIP), STRIP)
        return pltpu.make_async_copy(out_strip.at[r], out.at[:, :, rows, :], out_sem.at[r])

    @pl.loop(0, STEPS)
    def _(r):
        far_copy(r).wait_recv()
        out_strip[r] = (kept[r] + far_in[r].astype(F32)).astype(BF)
        out_copy(r).start()

    @pl.loop(0, CHUNKS)
    def _(q):
        for s in range(1, PARTS):
            in_copy(q, s).wait_send()
        row_copy(q, 0).wait_send()
        row_copy(q, 1).wait_send()

    @pl.loop(0, PAIRS)
    def _(p):
        for s in range(1, PARTS):
            back_copy(p, s).wait_send()

    for s in range(1, 4):
        meta_copy(s).wait_send()
        for late in range(2):
            for kind in range(2):
                x_copy(late, kind, s).wait_send()
    for r in range(STEPS):
        for late in range(2):
            core_copy(late, r).wait_send()
        far_copy(r).wait_send()
        out_copy(r).wait()


def body(green_blocks, coupling, phonon_weight, offsets, bond_atom):
    green = green_blocks.reshape(BONDS, 2, N, N)
    vmem, smem, dma = pltpu.VMEM, pltpu.SMEM, pltpu.SemaphoreType.DMA
    any_space = pl.BlockSpec(memory_space=pl.ANY)
    part = vmem((PARTS, BONDS, 2, ROWS, N), BF)
    out = pl.pallas_call(
        kernel,
        out_shape=jax.ShapeDtypeStruct((ATOMS, 2, N, N), BF),
        in_specs=[any_space] * 5,
        out_specs=any_space,
        scratch_shapes=[
            part, part, part, part,
            vmem((BONDS, 2, N, N), BF),
            vmem((BONDS, 3, 2, N, N), BF),
            vmem((BONDS, 2, N, N), BF),
            vmem((2, 2, 4, 2, 2, N, N), BF),
            vmem((2, 2, 4, 2, 2, N, N), BF),
            vmem((4, 2, 2, 2, 8, N), F32),
            vmem((4, 2, 2, 2, 8, N), F32),
            vmem((2, STEPS, ATOMS, 2, STRIP, N), BF),
            vmem((2, STEPS, ATOMS, 2, STRIP, N), BF),
            vmem((STEPS, ATOMS, 2, STRIP, N), F32),
            vmem((STEPS, ATOMS, 2, STRIP, N), BF),
            vmem((STEPS, ATOMS, 2, STRIP, N), BF),
            vmem((STEPS, ATOMS, 2, STRIP, N), BF),
            smem((2, MODES, BONDS), F32), smem((MODES, BONDS), jnp.int32), smem((BONDS,), jnp.int32),
            smem((BONDS,), jnp.int32), smem((BONDS,), jnp.int32), smem((BONDS,), jnp.int32),
            smem((OWNERS, 2), jnp.int32), smem((BONDS, 2 * MODES), F32),
            dma((3,)), dma((CHUNKS, PARTS)), dma((CHUNKS, PARTS)),
            dma((CHUNKS, 2)), dma((CHUNKS, 2)),
            dma((PAIRS, PARTS)), dma((PAIRS, PARTS)),
            dma, dma((PAIRS,)), dma,
            dma((4,)), dma((4,)),
            dma((2, 2, 4)), dma((2, 2, 4)),
            dma((2, STEPS)), dma((2, STEPS)),
            dma((STEPS,)), dma((STEPS,)), dma((STEPS,)),
        ],
        compiler_params=pltpu.CompilerParams(
            collective_id=0, has_side_effects=True, vmem_limit_bytes=63 * 1024 * 1024
        ),
    )(green, coupling, phonon_weight.transpose(0, 2, 1), offsets.T, bond_atom)
    return out.reshape(ATOMS, 1, 2, N, N)


def solution(mesh):
    placed = (
        P("atom", "energy", None, None, None),
        P("atom", None, None, None, None),
        P(None, "atom", None),
        P("atom", None),
        P("atom"),
    )
    return jax.shard_map(
        body,
        mesh=mesh,
        in_specs=placed,
        out_specs=P("atom", "energy", None, None, None),
        check_vma=False,
    )
```
